32 devices in a mesh: layer: 4 (over y, x), lat: 8 (over z, core).
Axes of the slice: x: 2, y: 2, z: 4, core: 2. Of those that a mesh axis runs over, the one named last changes fastest.
Arguments:
- activations: bfloat16 [8, 512, 2048], P(None, None, 'layer'), may hold values from -6 to 6
- targets: bfloat16 [8, 512, 2048], P(None, None, 'layer'), may hold values from -6 to 6
- encoder: bfloat16 [8, 2048, 8192], P(None, 'layer', 'lat'), may hold values from -0.125 to 0.125
- bias: float32 [8, 8192], P(None, 'lat'), may hold values from -3 to 3
- decoder: bfloat16 [36, 8192, 2048], P(None, 'lat', 'layer'), may hold values from -0.75 to 0.75
- active: int32 [8, 512, 64], replicated, may hold values from 0 to 8191, all different within a row
Outputs:
- grad_encoder: bfloat16 [8, 2048, 8192], P(None, 'layer', 'lat')
- grad_bias: float32 [8, 8192], P(None, 'lat')
- grad_decoder: bfloat16 [36, 8192, 2048], P(None, 'lat', 'layer')
The draws below stay inside these ranges and needn't reach their ends.
Inputs may be any that keep to these rules, and one draw needn't show every extreme that they name: `active`: each row names 64 different latents.
All inputs are finite; a program needn't handle non-finite values.
Results may differ from the reference program's by a relative error of at most 0.0064.
Values may be sent and summed in bfloat16 or wider, within the bound.
A program may use at most 256 MiB of HBM per device.

```python
import jax
import jax.numpy as jnp
from jax import lax

D = 2048
F = 8192
K = 64
LAYERS = 8
TOKENS = 512
PAIRS = 36


def shard_levels(key, dims, cuts, least, largest):
    def one(axis_at, parts):
        draws = jax.random.uniform(jax.random.fold_in(jax.random.fold_in(key, 6), axis_at), (parts,), jnp.float32, least / len(cuts), largest / len(cuts))
        return jnp.repeat(jnp.exp(draws), dims[axis_at] // parts).reshape((-1,) + (1,) * (len(dims) - axis_at - 1))

    gain = one(*cuts[0])
    for cut in cuts[1:]:
        gain = gain * one(*cut)
    return gain


def picks_of(rng, rows, count, top, lift):
    order = jax.random.permutation(jax.random.fold_in(rng, 1), count)
    favour = order
    for power in range(3):
        favour = favour * favour // count
    favour = favour * lift // count
    lots = jax.random.randint(jax.random.fold_in(rng, 2), (rows, count), 0, 4096) + favour
    sure = jax.random.permutation(jax.random.fold_in(rng, 3), rows)[jnp.arange(count) % rows]
    lots = jnp.where(jnp.arange(rows)[:, None] == sure[None, :], 1 << 14, lots)
    merit = lots * count + jnp.arange(count)
    return lax.top_k(merit.astype(jnp.int32), top)[1].astype(jnp.int32)


def bell_draw(key, shape, deviation, bound, shards=(), held_as=jnp.bfloat16):
    loudness = shard_levels(key, shape, shards, -0.22, 0.18) if shards else 1.0
    array = jax.random.normal(key, shape, jnp.float32) * deviation * loudness
    return jnp.minimum(jnp.maximum(array, -bound), bound).astype(held_as)


def setup_inputs(seed: int = 0) -> dict:
    seeds = jax.random.split(jax.random.key(seed), 7)
    activations = bell_draw(seeds[0], (LAYERS, TOKENS, D), 1.0, 6.0, ((2, 4),))
    targets = bell_draw(seeds[1], (LAYERS, TOKENS, D), 1.0, 6.0, ((2, 4),))
    encoder = bell_draw(seeds[2], (LAYERS, D, F), D ** -0.5, 0.125, ((1, 4), (2, 8)))
    bias = bell_draw(seeds[3], (LAYERS, F), 0.5, 3.0, ((1, 8),), jnp.float32)
    decoder = bell_draw(seeds[4], (PAIRS, F, D), K ** -0.5, 0.75, ((1, 8), (2, 4)))
    active = picks_of(seeds[5], LAYERS * TOKENS, F, K, 128).reshape((LAYERS, TOKENS, K))
    return {"activations": activations, "targets": targets, "encoder": encoder, "bias": bias, "decoder": decoder, "active": active}


def pair_index(source, target):
    return source * LAYERS - source * (source - 1) // 2 + (target - source)


def reference(activations, targets, encoder, bias, decoder, active):
    token_ids = jnp.arange(TOKENS, dtype=jnp.int32)
    masks = []
    latent_act = []
    for source in range(LAYERS):
        layer_mask = jnp.zeros((TOKENS, F), jnp.float32).at[token_ids[:, None], active[source]].set(1.0)
        preact = jnp.dot(activations[source], encoder[source], preferred_element_type=jnp.float32) + bias[source][None, :]
        masks.append(layer_mask)
        latent_act.append((preact * layer_mask).astype(jnp.bfloat16))
    errors = []
    for target in range(LAYERS):
        rebuilt = jnp.zeros((TOKENS, D), jnp.float32)
        for source in range(target + 1):
            rebuilt = rebuilt + jnp.dot(latent_act[source], decoder[pair_index(source, target)], preferred_element_type=jnp.float32)
        errors.append((rebuilt - targets[target].astype(jnp.float32)).astype(jnp.bfloat16))
    grad_decoder = []
    for source in range(LAYERS):
        for target in range(source, LAYERS):
            grad_decoder.append(jnp.dot(latent_act[source].T, errors[target], preferred_element_type=jnp.float32).astype(jnp.bfloat16))
    grad_encoder = []
    grad_bias = []
    for source in range(LAYERS):
        grad_act = jnp.zeros((TOKENS, F), jnp.float32)
        for target in range(source, LAYERS):
            grad_act = grad_act + jnp.dot(errors[target], decoder[pair_index(source, target)].T, preferred_element_type=jnp.float32)
        grad_pre = (grad_act * masks[source]).astype(jnp.bfloat16)
        grad_encoder.append(jnp.dot(activations[source].T, grad_pre, preferred_element_type=jnp.float32).astype(jnp.bfloat16))
        grad_bias.append(jnp.sum(grad_pre.astype(jnp.float32), axis=0))
    return jnp.stack(grad_encoder), jnp.stack(grad_bias), jnp.stack(grad_decoder)
```

```python
import functools

import jax
import jax.numpy as jnp
import numpy as np
from jax import lax
from jax.experimental import pallas as pl
from jax.experimental.pallas import tpu as pltpu
from jax.sharding import PartitionSpec as P

LANES = 128
FIELD = 7
PER_WORD = 4
GROUPS = ((7, 6), (5, 4), (3, 2, 1, 0))


def pair_index(source, target, layers):
    return source * layers - source * (source - 1) // 2 + (target - source)


def params(**kw):
    return pltpu.CompilerParams(vmem_limit_bytes=60 * 1024 * 1024, **kw)


def cost(flops, moved):
    return pl.CostEstimate(flops=int(flops), bytes_accessed=int(moved), transcendentals=0)


def pick(dense_block, index):
    lane = index & (LANES - 1)
    block = index >> 7
    value = jnp.zeros(index.shape, jnp.float32)
    for b in range(dense_block.shape[1] // LANES):
        part = dense_block[:, b * LANES : (b + 1) * LANES]
        got = jnp.take_along_axis(part, lane, axis=1, mode="promise_in_bounds")
        value = jnp.where(block == b, got, value)
    return value


def store_half(out_ref, rows, value, odd):
    half = lax.broadcasted_iota(jnp.int32, value.shape, 1) // (LANES // 2)
    mine = half == odd

    @pl.when(odd == 0)
    def _():
        out_ref[0, rows, :] = jnp.where(mine, value, 0.0)

    @pl.when(odd == 1)
    def _():
        out_ref[0, rows, :] = jnp.where(mine, value, out_ref[0, rows, :])


def encode_kernel(act_ref, enc_ref, bias_ref, index_ref, out_ref):
    odd = pl.program_id(0) % 2
    step = 128

    @pl.loop(0, act_ref.shape[1] // step)
    def _(i):
        rows = pl.ds(pl.multiple_of(i * step, step), step)
        pre = jnp.dot(act_ref[0, rows, :], enc_ref[0], preferred_element_type=jnp.float32)
        pre = pre + bias_ref[0]
        store_half(out_ref, rows, pick(pre, index_ref[0, rows, :]), odd)


def encode(act, enc, bias, index2):
    layers, tokens, width = act.shape
    lat = enc.shape[2]
    return pl.pallas_call(
        encode_kernel,
        grid=(layers,),
        in_specs=[
            pl.BlockSpec((1, tokens, width), lambda l: (l, 0, 0)),
            pl.BlockSpec((1, width, lat), lambda l: (l, 0, 0)),
            pl.BlockSpec((1, 1, lat), lambda l: (l, 0, 0)),
            pl.BlockSpec((1, tokens, LANES), lambda l: (l // 2, 0, 0)),
        ],
        out_specs=pl.BlockSpec((1, tokens, LANES), lambda l: (l // 2, 0, 0)),
        out_shape=jax.ShapeDtypeStruct((layers // 2, tokens, LANES), jnp.float32),
        compiler_params=params(),
        cost_estimate=cost(2 * layers * tokens * width * lat, act.size * 2 + enc.size * 2),
        name="encode",
    )(act, enc, bias[:, None, :], index2)


def compact_kernel(dense_ref, index_ref, out_ref):
    odd = pl.program_id(0) % 2
    step = 64

    @pl.loop(0, dense_ref.shape[1] // step)
    def _(i):
        rows = pl.ds(pl.multiple_of(i * step, step), step)
        store_half(out_ref, rows, pick(dense_ref[0, rows, :], index_ref[0, rows, :]), odd)


def compact(dense, index2):
    layers, tokens, lat = dense.shape
    return pl.pallas_call(
        compact_kernel,
        grid=(layers,),
        in_specs=[
            pl.BlockSpec((1, tokens, lat), lambda l: (l, 0, 0)),
            pl.BlockSpec((1, tokens, LANES), lambda l: (l // 2, 0, 0)),
        ],
        out_specs=pl.BlockSpec((1, tokens, LANES), lambda l: (l // 2, 0, 0)),
        out_shape=jax.ShapeDtypeStruct((layers // 2, tokens, LANES), jnp.float32),
        compiler_params=params(),
        cost_estimate=cost(0, dense.size * 4),
        name="compact",
    )(dense, index2)


def slots_kernel(words, blocks, index_ref, out_ref, *scratch):
    row_ref, code_refs = scratch[0], scratch[1:]
    tokens = index_ref.shape[2]
    slots = index_ref.shape[1]

    @pl.loop(0, tokens // LANES)
    def _(c):
        cols = pl.ds(pl.multiple_of(c * LANES, LANES), LANES)
        index = index_ref[0, :, cols]
        block = index >> 7
        local = (index >= 0) & (block < blocks)
        row_ref[...] = jnp.where(local, index & (LANES - 1), -1)
        code = (lax.broadcasted_iota(jnp.int32, index.shape, 0) + 1) << (FIELD * (block & (PER_WORD - 1)))
        for w in range(words):
            code_refs[w][...] = jnp.where((block >> 2) == w, code, 0)
        rows = lax.broadcasted_iota(jnp.int32, (LANES, LANES), 0)
        totals = [jnp.zeros((LANES, LANES), jnp.int32) for _ in range(words)]
        for k in range(slots):
            same = row_ref[k : k + 1, :] == rows
            for w in range(words):
                totals[w] = totals[w] | jnp.where(same, code_refs[w][k : k + 1, :], 0)
        for w in range(words):
            out_ref[0, w, cols, :] = totals[w].T


def slot_table(index_t, lat):
    layers, slots, tokens = index_t.shape
    blocks = lat // LANES
    words = -(-blocks // PER_WORD)
    return pl.pallas_call(
        functools.partial(slots_kernel, words, blocks),
        grid=(layers,),
        in_specs=[pl.BlockSpec((1, slots, tokens), lambda l: (l, 0, 0))],
        out_specs=pl.BlockSpec((1, words, tokens, LANES), lambda l: (l, 0, 0, 0)),
        out_shape=jax.ShapeDtypeStruct((layers, words, tokens, LANES), jnp.int32),
        scratch_shapes=[pltpu.VMEM((slots, LANES), jnp.int32)] * (1 + words),
        compiler_params=params(),
        cost_estimate=cost(2e10, 1e6),
        name="slot_table",
    )(index_t)


def spread(packed_ref, table_ref, rows, b, odd):
    field = (table_ref[0, b // PER_WORD, rows, :] >> (FIELD * (b % PER_WORD))) & (2**FIELD - 1)
    lane = jnp.maximum(field - 1, 0) + odd * (LANES // 2)
    packed = packed_ref[0, rows, :].astype(jnp.float32)
    got = jnp.take_along_axis(packed, lane, axis=1, mode="promise_in_bounds")
    return jnp.where(field > 0, got, 0.0)


def expand_kernel(packed_ref, table_ref, out_ref, flipped_ref):
    odd = pl.program_id(0) % 2
    tokens = packed_ref.shape[1]

    @pl.loop(0, tokens // LANES)
    def _(i):
        rows = pl.ds(pl.multiple_of(i * LANES, LANES), LANES)
        for b in range(out_ref.shape[2] // LANES):
            value = spread(packed_ref, table_ref, rows, b, odd)
            cols = slice(b * LANES, (b + 1) * LANES)
            out_ref[0, rows, cols] = value.astype(jnp.bfloat16)
            flipped_ref[0, cols, rows] = value.T.astype(jnp.bfloat16)


def expand(packed, table, lat):
    layers, words, tokens, _ = table.shape
    return pl.pallas_call(
        expand_kernel,
        grid=(layers,),
        in_specs=[
            pl.BlockSpec((1, tokens, LANES), lambda l: (l // 2, 0, 0)),
            pl.BlockSpec((1, words, tokens, LANES), lambda l: (l, 0, 0, 0)),
        ],
        out_specs=[
            pl.BlockSpec((1, tokens, lat), lambda l: (l, 0, 0)),
            pl.BlockSpec((1, lat, tokens), lambda l: (l, 0, 0)),
        ],
        out_shape=[
            jax.ShapeDtypeStruct((layers, tokens, lat), jnp.bfloat16),
            jax.ShapeDtypeStruct((layers, lat, tokens), jnp.bfloat16),
        ],
        compiler_params=params(),
        cost_estimate=cost(0, 4 * layers * tokens * lat),
        name="expand",
    )(packed, table)


def encoder_grad_kernel(packed_ref, table_ref, act_ref, grad_ref, bias_ref, dense_ref):
    odd = pl.program_id(0) % 2
    tokens = packed_ref.shape[1]
    lat = dense_ref.shape[1]
    bias_ref[...] = jnp.zeros_like(bias_ref)

    @pl.loop(0, tokens // LANES)
    def _(i):
        rows = pl.ds(pl.multiple_of(i * LANES, LANES), LANES)
        for b in range(lat // LANES):
            value = spread(packed_ref, table_ref, rows, b, odd)
            cols = slice(b * LANES, (b + 1) * LANES)
            dense_ref[rows, cols] = value.astype(jnp.bfloat16)
            bias_ref[0, :, cols] += jnp.sum(value, axis=0, keepdims=True)

    step = 256

    @pl.loop(0, lat // step)
    def _(j):
        cols = pl.ds(pl.multiple_of(j * step, step), step)
        grad_ref[0, :, cols] = lax.dot_general(
            act_ref[0], dense_ref[:, cols], (((0,), (0,)), ((), ())), preferred_element_type=jnp.float32
        ).astype(jnp.bfloat16)


def encoder_grad(packed, table, act, lat):
    layers, words, tokens, _ = table.shape
    width = act.shape[2]
    return pl.pallas_call(
        encoder_grad_kernel,
        grid=(layers,),
        in_specs=[
            pl.BlockSpec((1, tokens, LANES), lambda l: (l // 2, 0, 0)),
            pl.BlockSpec((1, words, tokens, LANES), lambda l: (l, 0, 0, 0)),
            pl.BlockSpec((1, tokens, width), lambda l: (l, 0, 0)),
        ],
        out_specs=[
            pl.BlockSpec((1, width, lat), lambda l: (l, 0, 0)),
            pl.BlockSpec((1, 1, lat), lambda l: (l, 0, 0)),
        ],
        out_shape=[
            jax.ShapeDtypeStruct((layers, width, lat), jnp.bfloat16),
            jax.ShapeDtypeStruct((layers, 1, lat), jnp.float32),
        ],
        scratch_shapes=[pltpu.VMEM((tokens, lat), jnp.bfloat16)],
        compiler_params=params(),
        cost_estimate=cost(2 * layers * tokens * width * lat, 4 * layers * width * lat),
        name="encoder_grad",
    )(packed, table, act)


def group_tables(group, layers):
    rows = [
        (source, place, pair_index(source, target, layers), int(source == target))
        for source in range(max(group) + 1)
        for place, target in enumerate(group)
        if target >= source
    ]
    return np.array(rows, np.int32)


def decode_kernel(tab_ref, lat_ref, dec_ref, out_ref, total_ref):
    i = pl.program_id(0)
    source, place, last = tab_ref[i, 0], tab_ref[i, 1], tab_ref[i, 3]
    step = 256

    @pl.loop(0, dec_ref.shape[2] // step)
    def _(j):
        cols = pl.ds(pl.multiple_of(j * step, step), step)
        part = jnp.dot(lat_ref[0], dec_ref[0, :, cols], preferred_element_type=jnp.float32)

        @pl.when(source == 0)
        def _():
            total_ref[place, :, cols] = part

        @pl.when(source > 0)
        def _():
            total_ref[place, :, cols] += part

    @pl.when(last == 1)
    def _():
        out_ref[place] = total_ref[place].astype(jnp.bfloat16)


def decode(group, lats, decoder):
    layers, tokens, lat = lats.shape
    width = decoder.shape[2]
    tab = group_tables(group, layers)
    shape = (len(group), tokens, width)
    return pl.pallas_call(
        decode_kernel,
        grid_spec=pltpu.PrefetchScalarGridSpec(
            num_scalar_prefetch=1,
            grid=(len(tab),),
            in_specs=[
                pl.BlockSpec((1, tokens, lat), lambda i, t: (t[i, 0], 0, 0)),
                pl.BlockSpec((1, lat, width), lambda i, t: (t[i, 2], 0, 0)),
            ],
            out_specs=pl.BlockSpec(shape, lambda i, t: (0, 0, 0)),
            scratch_shapes=[pltpu.VMEM(shape, jnp.float32)],
        ),
        out_shape=jax.ShapeDtypeStruct(shape, jnp.bfloat16),
        compiler_params=params(),
        cost_estimate=cost(2 * len(tab) * tokens * lat * width, 3 * len(tab) * lat * width),
        name="decode",
    )(jnp.asarray(tab), lats, decoder)


def backward_kernel(first_group, tab_ref, err_ref, flipped_ref, dec_ref, *rest):
    if first_group:
        act_ref, grad_ref = rest
    else:
        before_ref, _, act_ref, grad_ref = rest
    i = pl.program_id(0)
    place, fresh = tab_ref[i, 1], tab_ref[i, 4]
    step = 256

    @pl.loop(0, dec_ref.shape[1] // step)
    def _(j):
        cols = pl.ds(pl.multiple_of(j * step, step), step)
        grad_ref[0, cols, :] = jnp.dot(
            flipped_ref[0, cols, :], err_ref[place], preferred_element_type=jnp.float32
        ).astype(jnp.bfloat16)
        part = lax.dot_general(
            err_ref[place], dec_ref[0, cols, :], (((1,), (1,)), ((), ())), preferred_element_type=jnp.float32
        )

        @pl.when(fresh == 1)
        def _():
            act_ref[0, :, cols] = part if first_group else part + before_ref[0, :, cols]

        @pl.when(fresh == 0)
        def _():
            act_ref[0, :, cols] += part


def backward(group, errors, flipped, decoder, before, grads):
    layers, lat, tokens = flipped.shape
    pairs, _, width = decoder.shape
    tab = group_tables(group, layers)
    fresh = np.concatenate([[1], (np.diff(tab[:, 0]) != 0).astype(np.int32)])[:, None]
    tab = np.concatenate([tab, fresh], axis=1).astype(np.int32)
    act_spec = pl.BlockSpec((1, tokens, lat), lambda i, t: (t[i, 0], 0, 0))
    pair_spec = pl.BlockSpec((1, lat, width), lambda i, t: (t[i, 2], 0, 0))
    first = before is None
    in_specs = [
        pl.BlockSpec(errors.shape, lambda i, t: (0, 0, 0)),
        pl.BlockSpec((1, lat, tokens), lambda i, t: (t[i, 0], 0, 0)),
        pair_spec,
    ]
    operands = [jnp.asarray(tab), errors, flipped, decoder]
    if not first:
        in_specs += [act_spec, pl.BlockSpec(memory_space=pl.ANY)]
        operands += [before, grads]
    return pl.pallas_call(
        functools.partial(backward_kernel, first),
        grid_spec=pltpu.PrefetchScalarGridSpec(
            num_scalar_prefetch=1,
            grid=(len(tab),),
            in_specs=in_specs,
            out_specs=[act_spec, pair_spec],
        ),
        out_shape=[
            jax.ShapeDtypeStruct((layers, tokens, lat), jnp.float32),
            jax.ShapeDtypeStruct((pairs, lat, width), jnp.bfloat16),
        ],
        input_output_aliases={} if first else {4: 0, 5: 1},
        compiler_params=params(),
        cost_estimate=cost(4 * len(tab) * tokens * lat * width, 8 * len(tab) * lat * width),
        name="backward",
    )(*operands)


def exchange(packed):
    shape = packed.shape
    rows = packed.reshape((-1, shape[-1]))
    share = lax.psum_scatter(rows, "layer", scatter_dimension=0, tiled=True)
    return lax.all_gather(share.astype(jnp.bfloat16), "layer", axis=0, tiled=True).reshape(shape)


def on_device(activations, targets, encoder, bias, decoder, active):
    layers, tokens, slots = active.shape
    lat = encoder.shape[2]
    index = active - lax.axis_index("lat") * lat
    index2 = index.reshape((layers // 2, 2, tokens, slots)).transpose((0, 2, 1, 3))
    index2 = index2.reshape((layers // 2, tokens, 2 * slots))
    index_t = jnp.swapaxes(index, 1, 2)
    once = jnp.where(lax.axis_index("layer") == 0, bias, 0.0)
    packed = exchange(encode(activations, encoder, once, index2))
    table = slot_table(index_t, lat)
    lats, flipped = expand(packed, table, lat)
    groups = [tuple(m for m in group if m < layers) for group in GROUPS]
    summed = []
    for group in groups:
        partial = decode(group, lats, decoder)
        if summed:
            partial, summed[-1] = lax.optimization_barrier((partial, summed[-1]))
        summed.append(lax.psum(partial, "lat"))
    act = grads = None
    for group, complete in zip(groups, summed):
        wanted = jnp.stack([targets[m] for m in group])
        errors = (complete.astype(jnp.float32) - wanted.astype(jnp.float32)).astype(jnp.bfloat16)
        act, grads = backward(group, errors, flipped, decoder, act, grads)
    packed_grad = exchange(compact(act, index2))
    grad_encoder, grad_bias = encoder_grad(packed_grad, table, activations, lat)
    return (grad_encoder, grad_bias[:, 0, :], grads)


def solution(mesh):
    placed = (
        P(None, None, "layer"),
        P(None, None, "layer"),
        P(None, "layer", "lat"),
        P(None, "lat"),
        P(None, "lat", "layer"),
        P(),
    )
    return jax.shard_map(
        on_device,
        mesh=mesh,
        in_specs=placed,
        out_specs=(P(None, "layer", "lat"), P(None, "lat"), P(None, "lat", "layer")),
        check_vma=False,
    )
```

```python
import functools

import jax
import jax.numpy as jnp
import numpy as np
from jax import lax
from jax.experimental import pallas as pl
from jax.experimental.pallas import tpu as pltpu
from jax.sharding import PartitionSpec as P

LANES = 128
FIELD = 7
PER_WORD = 4


def pair_index(source, target, layers):
    return source * layers - source * (source - 1) // 2 + (target - source)


def params(**kw):
    return pltpu.CompilerParams(vmem_limit_bytes=60 * 1024 * 1024, **kw)


def cost(flops, moved):
    return pl.CostEstimate(flops=int(flops), bytes_accessed=int(moved), transcendentals=0)


def pick(dense_block, index):
    lane = index & (LANES - 1)
    block = index >> 7
    value = jnp.zeros(index.shape, jnp.float32)
    for b in range(dense_block.shape[1] // LANES):
        part = dense_block[:, b * LANES : (b + 1) * LANES]
        got = jnp.take_along_axis(part, lane, axis=1, mode="promise_in_bounds")
        value = jnp.where(block == b, got, value)
    return value


def store_half(out_ref, rows, value, odd):
    half = lax.broadcasted_iota(jnp.int32, value.shape, 1) // (LANES // 2)
    mine = half == odd

    @pl.when(odd == 0)
    def _():
        out_ref[0, rows, :] = jnp.where(mine, value, 0.0)

    @pl.when(odd == 1)
    def _():
        out_ref[0, rows, :] = jnp.where(mine, value, out_ref[0, rows, :])


def encode_kernel(act_ref, enc_ref, bias_ref, index_ref, out_ref):
    odd = pl.program_id(0) % 2
    step = 128

    @pl.loop(0, act_ref.shape[1] // step)
    def _(i):
        rows = pl.ds(pl.multiple_of(i * step, step), step)
        pre = jnp.dot(act_ref[0, rows, :], enc_ref[0], preferred_element_type=jnp.float32)
        pre = pre + bias_ref[0]
        store_half(out_ref, rows, pick(pre, index_ref[0, rows, :]), odd)


def encode(act, enc, bias, index2):
    layers, tokens, width = act.shape
    lat = enc.shape[2]
    return pl.pallas_call(
        encode_kernel,
        grid=(layers,),
        in_specs=[
            pl.BlockSpec((1, tokens, width), lambda l: (l, 0, 0)),
            pl.BlockSpec((1, width, lat), lambda l: (l, 0, 0)),
            pl.BlockSpec((1, 1, lat), lambda l: (l, 0, 0)),
            pl.BlockSpec((1, tokens, LANES), lambda l: (l // 2, 0, 0)),
        ],
        out_specs=pl.BlockSpec((1, tokens, LANES), lambda l: (l // 2, 0, 0)),
        out_shape=jax.ShapeDtypeStruct((layers // 2, tokens, LANES), jnp.float32),
        compiler_params=params(),
        cost_estimate=cost(2 * layers * tokens * width * lat, act.size * 2 + enc.size * 2),
        name="encode",
    )(act, enc, bias[:, None, :], index2)


def compact_kernel(dense_ref, index_ref, out_ref):
    odd = pl.program_id(0) % 2
    step = 64

    @pl.loop(0, dense_ref.shape[1] // step)
    def _(i):
        rows = pl.ds(pl.multiple_of(i * step, step), step)
        store_half(out_ref, rows, pick(dense_ref[0, rows, :], index_ref[0, rows, :]), odd)


def compact(dense, index2, first, count):
    _, tokens, lat = dense.shape
    return pl.pallas_call(
        compact_kernel,
        grid=(count,),
        in_specs=[
            pl.BlockSpec((1, tokens, lat), lambda l: (first + l, 0, 0)),
            pl.BlockSpec((1, tokens, LANES), lambda l: ((first + l) // 2, 0, 0)),
        ],
        out_specs=pl.BlockSpec((1, tokens, LANES), lambda l: (l // 2, 0, 0)),
        out_shape=jax.ShapeDtypeStruct((count // 2, tokens, LANES), jnp.float32),
        compiler_params=params(),
        cost_estimate=cost(0, count * tokens * lat * 16),
        name="compact",
    )(dense, index2)


def slots_kernel(words, blocks, *refs):
    index_ref = refs[0]
    out_ref, row_ref, *code_refs = refs[-2 - words :]
    tokens = index_ref.shape[2]
    slots = index_ref.shape[1]

    @pl.loop(0, tokens // LANES)
    def _(c):
        cols = pl.ds(pl.multiple_of(c * LANES, LANES), LANES)
        index = index_ref[0, :, cols]
        block = index >> 7
        local = (index >= 0) & (block < blocks)
        slot = lax.broadcasted_iota(jnp.int32, index.shape, 0)
        entry = jnp.where(local, index | ((slot + 1) << 16), -1)
        ahead = jnp.where(local, 0, 1)
        step = 1
        while step < slots:
            ahead = ahead + jnp.where(slot >= step, pltpu.roll(ahead, step, 0), 0)
            step *= 2
        step = 1
        while step < slots:
            entry_below = pltpu.roll(entry, slots - step, 0)
            ahead_below = pltpu.roll(ahead, slots - step, 0)
            come = (entry_below >= 0) & ((ahead_below & step) != 0) & (slot < slots - step)
            go = (ahead & step) != 0
            entry = jnp.where(come, entry_below, jnp.where(go, -1, entry))
            ahead = jnp.where(come, ahead_below, ahead)
            step *= 2
        most = jnp.max(jnp.where(entry >= 0, slot + 1, 0))
        row_ref[...] = jnp.where(entry >= 0, entry & (LANES - 1), -1)
        block = (entry >> 7) & 511
        code = (entry >> 16) << (FIELD * (block & (PER_WORD - 1)))
        for w in range(words):
            code_refs[w][...] = jnp.where((entry >= 0) & ((block >> 2) == w), code, 0)
        rows = lax.broadcasted_iota(jnp.int32, (LANES, LANES), 0)
        unroll = 4

        def add(turn, totals):
            totals = list(totals)
            for u in range(unroll):
                k = pl.ds(turn * unroll + u, 1)
                same = row_ref[k, :] == rows
                for w in range(words):
                    totals[w] = totals[w] | jnp.where(same, code_refs[w][k, :], 0)
            return tuple(totals)

        start = tuple(jnp.zeros((LANES, LANES), jnp.int32) for _ in range(words))
        totals = lax.fori_loop(0, (most + unroll - 1) // unroll, add, start)
        for w in range(words):
            out_ref[0, w, cols, :] = totals[w].T


def slot_table(index_t, lat, first, count, before=None):
    layers, slots, tokens = index_t.shape
    blocks = lat // LANES
    words = -(-blocks // PER_WORD)
    kept = [] if before is None else [before]
    return pl.pallas_call(
        functools.partial(slots_kernel, words, blocks),
        grid=(count,),
        in_specs=[pl.BlockSpec((1, slots, tokens), lambda l: (first + l, 0, 0))]
        + [pl.BlockSpec(memory_space=pl.ANY)] * len(kept),
        out_specs=pl.BlockSpec((1, words, tokens, LANES), lambda l: (first + l, 0, 0, 0)),
        out_shape=jax.ShapeDtypeStruct((layers, words, tokens, LANES), jnp.int32),
        input_output_aliases={1: 0} if kept else {},
        scratch_shapes=[pltpu.VMEM((slots, LANES), jnp.int32)] * (1 + words),
        compiler_params=params(),
        cost_estimate=cost(count * 2.5e9, 1e6),
        name="slot_table",
    )(index_t, *kept)


def spread(packed_ref, table_ref, rows, b, odd):
    field = (table_ref[0, b // PER_WORD, rows, :] >> (FIELD * (b % PER_WORD))) & (2**FIELD - 1)
    lane = jnp.maximum(field - 1, 0) + odd * (LANES // 2)
    packed = packed_ref[0, rows, :].astype(jnp.float32)
    got = jnp.take_along_axis(packed, lane, axis=1, mode="promise_in_bounds")
    return jnp.where(field > 0, got, 0.0)


def expand_kernel(packed_ref, table_ref, out_ref):
    odd = pl.program_id(0) % 2
    tokens = packed_ref.shape[1]

    @pl.loop(0, tokens // LANES)
    def _(i):
        rows = pl.ds(pl.multiple_of(i * LANES, LANES), LANES)
        for b in range(out_ref.shape[2] // LANES):
            value = spread(packed_ref, table_ref, rows, b, odd)
            out_ref[0, rows, b * LANES : (b + 1) * LANES] = value.astype(jnp.bfloat16)


def expand(packed, table, lat):
    layers, words, tokens, _ = table.shape
    return pl.pallas_call(
        expand_kernel,
        grid=(layers,),
        in_specs=[
            pl.BlockSpec((1, tokens, LANES), lambda l: (l // 2, 0, 0)),
            pl.BlockSpec((1, words, tokens, LANES), lambda l: (l, 0, 0, 0)),
        ],
        out_specs=pl.BlockSpec((1, tokens, lat), lambda l: (l, 0, 0)),
        out_shape=jax.ShapeDtypeStruct((layers, tokens, lat), jnp.bfloat16),
        compiler_params=params(),
        cost_estimate=cost(0, 8 * layers * tokens * lat),
        name="expand",
    )(packed, table)


def flip_kernel(lat_ref, *refs):
    out_ref = refs[-1]
    for b in range(lat_ref.shape[2] // LANES):
        cols = slice(b * LANES, (b + 1) * LANES)
        out_ref[0, cols, :] = lat_ref[0, :, cols].T


def flip(lats, after):
    layers, tokens, lat = lats.shape
    return pl.pallas_call(
        flip_kernel,
        grid=(layers,),
        in_specs=[pl.BlockSpec((1, tokens, lat), lambda l: (l, 0, 0))] + [pl.BlockSpec(memory_space=pl.ANY)] * len(after),
        out_specs=pl.BlockSpec((1, lat, tokens), lambda l: (l, 0, 0)),
        out_shape=jax.ShapeDtypeStruct((layers, lat, tokens), jnp.bfloat16),
        compiler_params=params(),
        cost_estimate=cost(0, 4 * lats.size),
        name="flip",
    )(lats, *after)


def encoder_grad_kernel(packed_ref, table_ref, act_ref, *refs):
    grad_ref, bias_ref, dense_ref = refs[-3:]
    odd = pl.program_id(0) % 2
    tokens = packed_ref.shape[1]
    lat = dense_ref.shape[1]
    bias_ref[...] = jnp.zeros_like(bias_ref)

    @pl.loop(0, tokens // LANES)
    def _(i):
        rows = pl.ds(pl.multiple_of(i * LANES, LANES), LANES)
        for b in range(lat // LANES):
            value = spread(packed_ref, table_ref, rows, b, odd)
            cols = slice(b * LANES, (b + 1) * LANES)
            dense_ref[rows, cols] = value.astype(jnp.bfloat16)
            bias_ref[0, :, cols] += jnp.sum(value, axis=0, keepdims=True)

    step = 256

    @pl.loop(0, lat // step)
    def _(j):
        cols = pl.ds(pl.multiple_of(j * step, step), step)
        grad_ref[0, :, cols] = lax.dot_general(
            act_ref[0], dense_ref[:, cols], (((0,), (0,)), ((), ())), preferred_element_type=jnp.float32
        ).astype(jnp.bfloat16)


def encoder_grad(packed, table, act, lat, first, count, before, after):
    layers, words, tokens, _ = table.shape
    width = act.shape[2]
    kept = [] if before is None else list(before)
    return pl.pallas_call(
        encoder_grad_kernel,
        grid=(count,),
        in_specs=[
            pl.BlockSpec((1, tokens, LANES), lambda l: (l // 2, 0, 0)),
            pl.BlockSpec((1, words, tokens, LANES), lambda l: (first + l, 0, 0, 0)),
            pl.BlockSpec((1, tokens, width), lambda l: (first + l, 0, 0)),
        ]
        + [pl.BlockSpec(memory_space=pl.ANY)] * len(kept + after),
        out_specs=[
            pl.BlockSpec((1, width, lat), lambda l: (first + l, 0, 0)),
            pl.BlockSpec((1, 1, lat), lambda l: (first + l, 0, 0)),
        ],
        out_shape=[
            jax.ShapeDtypeStruct((layers, width, lat), jnp.bfloat16),
            jax.ShapeDtypeStruct((layers, 1, lat), jnp.float32),
        ],
        input_output_aliases={3: 0, 4: 1} if kept else {},
        scratch_shapes=[pltpu.VMEM((tokens, lat), jnp.bfloat16)],
        compiler_params=params(),
        cost_estimate=cost(4 * count * tokens * width * lat, 4 * count * width * lat),
        name="encoder_grad",
    )(packed, table, act, *kept, *after)


def group_tables(group, layers):
    rows = [
        (source, place, pair_index(source, target, layers), int(source == target))
        for source in range(max(group) + 1)
        for place, target in enumerate(group)
        if target >= source
    ]
    return np.array(rows, np.int32)


def decode_kernel(tab_ref, lat_ref, dec_ref, *refs):
    out_ref, total_ref = refs[-2:]
    i = pl.program_id(0)
    source, place, last = tab_ref[i, 0], tab_ref[i, 1], tab_ref[i, 3]
    part = jnp.dot(lat_ref[0], dec_ref[0], preferred_element_type=jnp.float32)

    @pl.when(source == 0)
    def _():
        total_ref[place] = part

    @pl.when(source > 0)
    def _():
        total_ref[place] += part

    @pl.when(last == 1)
    def _():
        out_ref[place] = total_ref[place].astype(jnp.bfloat16)


def decode(group, lats, decoder, after):
    layers, tokens, lat = lats.shape
    width = decoder.shape[2]
    tab = group_tables(group, layers)
    shape = (len(group), tokens, width)
    return pl.pallas_call(
        decode_kernel,
        grid_spec=pltpu.PrefetchScalarGridSpec(
            num_scalar_prefetch=1,
            grid=(len(tab),),
            in_specs=[
                pl.BlockSpec((1, tokens, lat), lambda i, t: (t[i, 0], 0, 0)),
                pl.BlockSpec((1, lat, width), lambda i, t: (t[i, 2], 0, 0)),
            ]
            + [pl.BlockSpec(memory_space=pl.ANY)] * len(after),
            out_specs=pl.BlockSpec(shape, lambda i, t: (0, 0, 0)),
            scratch_shapes=[pltpu.VMEM(shape, jnp.float32)],
        ),
        out_shape=jax.ShapeDtypeStruct(shape, jnp.bfloat16),
        compiler_params=params(),
        cost_estimate=cost(2 * len(tab) * tokens * lat * width, 3 * len(tab) * lat * width),
        name="decode",
    )(jnp.asarray(tab), lats, decoder, *after)


def backward_kernel(first_group, tab_ref, err_ref, flipped_ref, dec_ref, *rest):
    act_ref, grad_ref = rest[-2:]
    before_ref = rest[0]
    i = pl.program_id(0)
    place, fresh = tab_ref[i, 1], tab_ref[i, 4]
    grad_ref[0] = jnp.dot(flipped_ref[0], err_ref[place], preferred_element_type=jnp.float32).astype(jnp.bfloat16)
    part = lax.dot_general(
        err_ref[place], dec_ref[0], (((1,), (1,)), ((), ())), preferred_element_type=jnp.float32
    )

    @pl.when(fresh == 1)
    def _():
        act_ref[0] = part if first_group else part + before_ref[0]

    @pl.when(fresh == 0)
    def _():
        act_ref[0] += part


def backward(group, errors, flipped, decoder, before, grads, after):
    layers, lat, tokens = flipped.shape
    pairs, _, width = decoder.shape
    tab = group_tables(group, layers)
    fresh = np.concatenate([[1], (np.diff(tab[:, 0]) != 0).astype(np.int32)])[:, None]
    tab = np.concatenate([tab, fresh], axis=1).astype(np.int32)
    act_spec = pl.BlockSpec((1, tokens, lat), lambda i, t: (t[i, 0], 0, 0))
    pair_spec = pl.BlockSpec((1, lat, width), lambda i, t: (t[i, 2], 0, 0))
    first = before is None
    in_specs = [
        pl.BlockSpec(errors.shape, lambda i, t: (0, 0, 0)),
        pl.BlockSpec((1, lat, tokens), lambda i, t: (t[i, 0], 0, 0)),
        pair_spec,
    ]
    operands = [jnp.asarray(tab), errors, flipped, decoder]
    if not first:
        in_specs += [act_spec, pl.BlockSpec(memory_space=pl.ANY)]
        operands += [before, grads]
    in_specs += [pl.BlockSpec(memory_space=pl.ANY)] * len(after)
    operands += after
    return pl.pallas_call(
        functools.partial(backward_kernel, first),
        grid_spec=pltpu.PrefetchScalarGridSpec(
            num_scalar_prefetch=1,
            grid=(len(tab),),
            in_specs=in_specs,
            out_specs=[act_spec, pair_spec],
        ),
        out_shape=[
            jax.ShapeDtypeStruct((max(group) + 1, tokens, lat), jnp.float32),
            jax.ShapeDtypeStruct((pairs, lat, width), jnp.bfloat16),
        ],
        input_output_aliases={} if first else {5: 1},
        compiler_params=params(),
        cost_estimate=cost(4 * len(tab) * tokens * lat * width, 8 * len(tab) * lat * width),
        name="backward",
    )(*operands)


def scatter_sum(rows, own, dim, axis, shifts, places):
    place, count = places
    share = rows.shape[dim] // count
    total = lax.dynamic_slice_in_dim(own, place * share, share, dim)
    for shift in range(1, count):
        sent = lax.dynamic_slice_in_dim(rows, (place + shift) % count * share, share, dim)
        total = total + lax.ppermute(sent, axis, shifts(shift)).astype(jnp.float32)
    return total


def gather(share, dim, axis, shifts, places):
    place, count = places
    size = share.shape[dim]
    shape = share.shape[:dim] + (size * count,) + share.shape[dim + 1 :]
    full = jnp.zeros(shape, share.dtype)
    for shift in range(count):
        piece = share if shift == 0 else lax.ppermute(share, axis, shifts(shift))
        full = lax.dynamic_update_slice_in_dim(full, piece, (place - shift) % count * size, dim)
    return full


def layer_shifts():
    count = lax.axis_size("layer")
    return lambda s: [(j, (j + s) % count) for j in range(count)], (lax.axis_index("layer"), count)


def sum_share(packed):
    shifts, places = layer_shifts()
    rows = packed.reshape((-1, packed.shape[-1]))
    return scatter_sum(rows, rows, 0, "layer", shifts, places).astype(jnp.bfloat16)


def all_rows(share, shape):
    shifts, places = layer_shifts()
    return gather(share, 0, "layer", shifts, places).reshape(shape)


def lat_moves():
    count = lax.axis_size("lat")
    chips = count // 2
    swap = lambda s: [(j, j ^ 1) for j in range(count)]
    shifts = lambda s: [(j, (j // 2 + s) % chips * 2 + j % 2) for j in range(count)]
    return swap, (lax.axis_index("lat") % 2, 2), shifts, (lax.axis_index("lat") // 2, chips)


def sum_cores(partial):
    swap, core, _, _ = lat_moves()
    return scatter_sum(partial, partial.astype(jnp.float32), 1, "lat", swap, core)


def error_share(half, wanted):
    _, core, shifts, chip = lat_moves()
    total = scatter_sum(half.astype(jnp.bfloat16), half, 1, "lat", shifts, chip)
    rows = total.shape[1]
    mine = lax.dynamic_slice_in_dim(wanted, core[0] * half.shape[1] + chip[0] * rows, rows, 1)
    return (total - mine.astype(jnp.float32)).astype(jnp.bfloat16)


def half_errors(share):
    _, _, shifts, chip = lat_moves()
    return gather(share, 1, "lat", shifts, chip)


def all_errors(half):
    swap, core, _, _ = lat_moves()
    return gather(half, 1, "lat", swap, core)


def on_device(activations, targets, encoder, bias, decoder, active):
    layers, tokens, slots = active.shape
    lat = encoder.shape[2]
    mid = layers // 2
    index = active - lax.axis_index("lat") * lat
    index2 = index.reshape((layers // 2, 2, tokens, slots)).transpose((0, 2, 1, 3))
    index2 = index2.reshape((layers // 2, tokens, 2 * slots))
    index_t = jnp.swapaxes(index, 1, 2)
    once = jnp.where(lax.axis_index("layer") == 0, bias, 0.0)
    packed = encode(activations, encoder, once, index2)
    packed = all_rows(sum_share(packed), packed.shape)
    table = slot_table(index_t, lat, 0, mid)
    table = slot_table(index_t, lat, mid, layers - mid, table)
    lats = expand(packed, table, lat)
    groups = [(2 * j + 1, 2 * j) for j in reversed(range(layers // 2))]
    halves, shares = [], []
    count = len(groups)
    for at, group in enumerate(groups):
        after = ([halves[at - 2]] if at >= 2 else []) + ([shares[at - 3]] if at >= 3 else [])
        halves.append(sum_cores(decode(group, lats, decoder, after)))
        wanted = jnp.stack([targets[m] for m in group])
        shares.append(error_share(halves[-1], wanted))
    spread_errors = [half_errors(share) for share in shares]
    flipped = flip(lats, [spread_errors[0]] + shares[1:2] + halves[2:3])
    act = grads = grad_encoder = share = waiting = None
    finished = []
    for at, group in enumerate(groups):
        after = shares[at + 1 : at + 2] + halves[at + 2 : at + 4]
        if waiting is not None:
            after.append(waiting if share is None else share)
            share = sum_share(waiting) if share is None else share
        act, grads = backward(group, all_errors(spread_errors[at]), flipped, decoder, act, grads, after)
        finished.insert(0, compact(act, index2, min(group), len(group)))
        if min(group) == mid:
            waiting, finished = jnp.concatenate(finished), []
    last = jnp.concatenate(finished)
    share = sum_share(waiting) if share is None else share
    grad_encoder = encoder_grad(
        all_rows(share, waiting.shape), table, activations, lat, mid, layers - mid, None, [last]
    )
    last_rows = all_rows(sum_share(last), last.shape)
    grad_encoder = encoder_grad(last_rows, table, activations, lat, 0, mid, grad_encoder, [])
    return (grad_encoder[0], grad_encoder[1][:, 0, :], grads)


def solution(mesh):
    placed = (
        P(None, None, "layer"),
        P(None, None, "layer"),
        P(None, "layer", "lat"),
        P(None, "lat"),
        P(None, "lat", "layer"),
        P(),
    )
    return jax.shard_map(
        on_device,
        mesh=mesh,
        in_specs=placed,
        out_specs=(P(None, "layer", "lat"), P(None, "lat"), P(None, "lat", "layer")),
        check_vma=False,
    )
```
